32 devices in a mesh: dp: 2 (over x), row: 4 (over y, core), col: 4 (over z).
Axes of the slice: x: 2, y: 2, z: 4, core: 2. Of those that a mesh axis runs over, the one named last changes fastest.
Arguments:
- tokens: bfloat16 [6304, 512], P(('dp', 'row'), 'col'), may hold values from -9 to 9
- cotangent: bfloat16 [6304, 512], P(('dp', 'row'), 'col'), may hold values from -6 to 6
- expert_ids: int32 [6304, 2], P(('dp', 'row')), may hold values from 0 to 3, all different within a row
- priority: int32 [8, 788], P(('dp', 'row')), may hold values from 0 to 787, each once within a row
- qkv_weight: bfloat16 [512, 3, 512], P('col', None, 'row'), may hold values from -0.25 to 0.25
- out_weight: bfloat16 [512, 512], P('row', 'col'), may hold values from -2 to 2
- attn_gain: bfloat16 [512], P('col'), may hold values from 0.5 to 1.5
- attn_shift: bfloat16 [512], P('col'), may hold values from -0.5 to 0.5
- moe_gain: bfloat16 [512], P('col'), may hold values from 0.5 to 1.5
- moe_shift: bfloat16 [512], P('col'), may hold values from -0.5 to 0.5
- router: bfloat16 [512, 4], P('col'), may hold values from -0.1875 to 0.1875
- up_weight: bfloat16 [4, 512, 2048], P('dp', 'col', 'row'), may hold values from -0.25 to 0.25
- down_weight: bfloat16 [4, 2048, 512], P('dp', 'row', 'col'), may hold values from -0.1875 to 0.1875
Outputs:
- block_out: bfloat16 [6304, 512], P(('dp', 'row'), 'col')
- tokens_grad: bfloat16 [6304, 512], P(('dp', 'row'), 'col')
- qkv_grad: float32 [512, 3, 512], P('col', None, 'row')
- out_grad: float32 [512, 512], P('row', 'col')
- attn_gain_grad: float32 [512], P('col')
- attn_shift_grad: float32 [512], P('col')
- moe_gain_grad: float32 [512], P('col')
- moe_shift_grad: float32 [512], P('col')
- router_grad: float32 [512, 4], P('col')
- up_grad: float32 [4, 512, 2048], P('dp', 'col', 'row')
- down_grad: float32 [4, 2048, 512], P('dp', 'row', 'col')
- stream_rms: float32 [5], replicated
The draws below stay inside these ranges and needn't reach their ends.
Inputs may be any that keep to these rules, and one draw needn't show every extreme that they name: `expert_ids`: each row names 2 different experts. `priority`: each row holds every token index of its block of 788 tokens once.
All inputs are finite; a program needn't handle non-finite values.
Results may differ from the reference program's by a relative error of at most 0.014.
Values may be sent and summed in bfloat16 or wider, within the bound.
No kernel may reach another device: no remote copies, remote signals or barrier semaphores. Data moves between devices by JAX's collectives and lax.ppermute only.
A program may use at most 128 MiB of HBM per device.

```python
import jax
import jax.numpy as jnp
from jax import lax

D = 512
HEADS = 8
HDIM = 64
FF = 2048
SEQ = 197
E_DEV = 2
TOPK = 2
HD = 512
EXPERTS = 4
TOK_SH = 788
CAP = 496
TOKENS = 6304
IMAGES = 32
N_DP = 2
N_ROW = 4


def draw_tokens(key, part):
    base_values = jnp.clip(jax.random.normal(key, (TOKENS, D), jnp.float32), -5.0, 5.0)
    level = 0.6 * 3.0 ** (jnp.arange(TOKENS, dtype=jnp.float32) / TOKENS)
    return (base_values * level[:, None]).astype(jnp.bfloat16)


def shard_levels(rng, extent, split, smallest, high):
    level = 1.0
    for position, blocks in split:
        heights = jax.random.uniform(jax.random.fold_in(jax.random.fold_in(rng, 6), position), (blocks,), jnp.float32, smallest / len(split), high / len(split))
        level = level * jnp.repeat(jnp.exp(heights), extent[position] // blocks).reshape((-1,) + (1,) * (len(extent) - 1 - position))
    return level


def different_ones(key, rows, count, top, lift):
    sequence = jax.random.permutation(jax.random.fold_in(key, 1), count)
    favour = sequence
    for power in range(3):
        favour = favour * favour // count
    favour = favour * lift // count
    chance = jax.random.randint(jax.random.fold_in(key, 2), (rows, count), 0, 4096) + favour
    holders = jax.random.permutation(jax.random.fold_in(key, 3), rows)[jnp.arange(count) % rows]
    chance = jnp.where(jnp.arange(rows)[:, None] == holders[None, :], 1 << 14, chance)
    merit = chance * count + jnp.arange(count)
    return lax.top_k(merit.astype(jnp.int32), top)[1].astype(jnp.int32)


def gaussian(rng, extent, width, reach, split=(), kind=jnp.bfloat16):
    result = width * jax.random.normal(rng, extent, jnp.float32)
    if split:
        result = result * shard_levels(rng, extent, split, -0.22, 0.18)
    return jnp.clip(result, -reach, reach).astype(kind)


def setup_inputs(seed: int = 0) -> dict:
    seeds = jax.random.split(jax.random.key(seed), 14)
    tokens = draw_tokens(jax.random.fold_in(seeds[13], 71), 0)
    cotangent = gaussian(seeds[1], (TOKENS, D), 1.0, 6.0, ((0, 8), (1, 4)))
    expert_ids = different_ones(seeds[2], TOKENS, EXPERTS, TOPK, 4096)
    priority = jax.vmap(lambda own: jax.random.permutation(own, TOK_SH))(jax.random.split(seeds[3], (N_DP * N_ROW))).reshape((N_DP * N_ROW, TOK_SH)).astype(jnp.int32)
    qkv_weight = gaussian(seeds[4], (D, 3, HD), D ** -0.5, 0.25, ((0, 4), (2, 4)))
    out_weight = gaussian(seeds[5], (HD, D), (max(2, HD // 64)) ** -0.5, 2.0, ((0, 4), (1, 4)))
    attn_gain = jnp.clip(1.0 + 0.1 * jax.random.normal(seeds[6], (D,), jnp.float32), 0.5, 1.5).astype(jnp.bfloat16)
    attn_shift = gaussian(seeds[7], (D,), 0.1, 0.5, ((0, 4),))
    moe_gain = jnp.clip(1.0 + 0.1 * jax.random.normal(seeds[8], (D,), jnp.float32), 0.5, 1.5).astype(jnp.bfloat16)
    moe_shift = gaussian(seeds[9], (D,), 0.1, 0.5, ((0, 4),))
    router = gaussian(seeds[10], (D, EXPERTS), (2 * D) ** -0.5, 0.1875, ((0, 4),))
    up_weight = gaussian(seeds[11], (EXPERTS, D, FF), D ** -0.5, 0.25, ((0, 2), (1, 4), (2, 4)))
    down_weight = gaussian(seeds[12], (EXPERTS, FF, D), (FF // 2) ** -0.5, 0.1875, ((0, 2), (1, 4), (2, 4)))
    return dict(tokens=tokens, cotangent=cotangent, expert_ids=expert_ids, priority=priority, qkv_weight=qkv_weight, out_weight=out_weight, attn_gain=attn_gain, attn_shift=attn_shift, moe_gain=moe_gain, moe_shift=moe_shift, router=router, up_weight=up_weight, down_weight=down_weight)


@jax.custom_vjp
def low(v):
    return lax.optimization_barrier(v.astype(jnp.bfloat16)).astype(jnp.float32)

@jax.custom_vjp
def low_back(v):
    return v

def low_keep(v):
    return (low(v), None)

def low_pass(kept, grad):
    return (grad,)

def back_keep(v):
    return (v, None)

def back_low(kept, grad):
    return (low(grad),)
low.defvjp(low_keep, low_pass)
low_back.defvjp(back_keep, back_low)
epsilon = 1e-06

def product(left_side, right_side):
    return jnp.dot(left_side, right_side, precision=lax.Precision.HIGHEST, preferred_element_type=jnp.float32)

def normalize(values, norm_gain, norm_shift):
    center = values - lax.optimization_barrier(jnp.mean(values, axis=-1, keepdims=True))
    spread = lax.optimization_barrier(jnp.mean(center * center, axis=-1, keepdims=True))
    return center * lax.rsqrt(spread + epsilon) * norm_gain + norm_shift

def attend(pieces):
    queries = pieces[:, :, 0]
    key_rows = pieces[:, :, 1]
    values = pieces[:, :, 2]
    scores = jnp.einsum('bqhd,bkhd->bhqk', queries, key_rows, precision=lax.Precision.HIGHEST) * HDIM ** (-0.5)
    scores = low_back(scores)
    row_peak = lax.optimization_barrier(jnp.max(scores, axis=-1, keepdims=True))
    raised = jnp.exp(scores - row_peak)
    weights = raised / lax.optimization_barrier(jnp.sum(raised, axis=-1, keepdims=True))
    mixed_rows = jnp.einsum('bhqk,bkhd->bqhd', low(weights), values, precision=lax.Precision.HIGHEST)
    return mixed_rows.reshape(mixed_rows.shape[0], SEQ, HEADS * HDIM)

def expert(pieces):
    slot_inputs, up_block, down_block = pieces
    hidden_pre = low_back(product(slot_inputs, up_block))
    hidden = low(jax.nn.gelu(hidden_pre, approximate=False))
    return low(low_back(product(hidden, down_block)))

def placement(choice_ids, priority_row, experts, capacity):
    token_count = priority_row.shape[0]
    ranked = jnp.take(choice_ids, priority_row, axis=0)
    pair_expert = jnp.concatenate([ranked[:, 0], ranked[:, 1]])
    onehot = (pair_expert[:, None] == jnp.arange(experts, dtype=jnp.int32)[None, :]).astype(jnp.int32)
    earlier = (jnp.cumsum(onehot, axis=0) - onehot).astype(jnp.int32)
    slot_rank = lax.optimization_barrier(jnp.sum(earlier * onehot, axis=1)).astype(jnp.int32)
    slot_index = jnp.where(slot_rank < capacity, slot_rank * experts + pair_expert, experts * capacity).astype(jnp.int32)
    per_token = jnp.zeros((token_count, 2), jnp.int32).at[priority_row].set(jnp.stack([slot_index[:token_count], slot_index[token_count:]], axis=1))
    pair_index = jnp.arange(2 * token_count, dtype=jnp.int32)
    holder = jnp.full((experts * capacity,), 2 * token_count, jnp.int32).at[per_token.reshape(-1)].set(pair_index, mode='drop')
    return (per_token, holder)

def forward(stream, qkv_weight, out_weight, attn_gain, attn_shift, moe_gain, moe_shift, router, up_weight, down_weight, expert_ids, priority):
    groups = TOKENS // TOK_SH
    first_normed = low(normalize(stream, attn_gain, attn_shift))
    mixed_in = low(low_back(product(first_normed, qkv_weight.reshape(D, 3 * HEADS * HDIM))))
    blocks = mixed_in.reshape(IMAGES // 8, 8, SEQ, 3, HEADS, HDIM)
    attended = lax.map(jax.checkpoint(attend), blocks).reshape(TOKENS, HEADS * HDIM)
    attended = low(low_back(attended))
    branch = low_back(product(attended, out_weight))
    middle = stream + branch
    second_normed = low(normalize(middle, moe_gain, moe_shift))
    logits = low_back(product(second_normed, router))
    chosen = jnp.take_along_axis(logits, expert_ids, axis=1)
    raised = jnp.exp(chosen - lax.optimization_barrier(jnp.max(chosen, axis=1, keepdims=True)))
    gate_values = raised / lax.optimization_barrier(jnp.sum(raised, axis=1, keepdims=True))
    per_token, holder = jax.vmap(lambda ids_group, order_group: placement(ids_group, order_group, EXPERTS, CAP))(expert_ids.reshape(groups, TOK_SH, 2), priority)
    padded = jnp.concatenate([second_normed.reshape(groups, TOK_SH, D), jnp.zeros((groups, 1, D), jnp.float32)], axis=1)
    dispatched = jax.vmap(lambda group_rows, group_holder: group_rows[group_holder // 2])(padded, holder)
    dispatched = low_back(dispatched)
    stacked = dispatched.reshape(groups, CAP, N_DP, E_DEV, D).transpose(2, 3, 0, 1, 4).reshape(EXPERTS, groups * CAP, D)
    expert_outputs = lax.map(jax.checkpoint(expert), (stacked, up_weight, down_weight))
    returned = expert_outputs.reshape(N_DP, E_DEV, groups, CAP, D).transpose(2, 3, 0, 1, 4).reshape(groups, CAP * EXPERTS, D)
    returned = jnp.concatenate([returned, jnp.zeros((groups, 1, D), jnp.float32)], axis=1)
    picked = jax.vmap(lambda out_rows, slot_rows: out_rows[slot_rows])(returned, per_token).reshape(TOKENS, 2, D)
    mixture = lax.optimization_barrier(jnp.sum(gate_values[:, :, None] * picked, axis=1))
    output = middle + mixture
    return (output, (branch, middle, mixture))

def reference(tokens, cotangent, expert_ids, priority, qkv_weight, out_weight, attn_gain, attn_shift, moe_gain, moe_shift, router, up_weight, down_weight):
    floats = tuple((value.astype(jnp.float32) for value in (tokens, qkv_weight, out_weight, attn_gain, attn_shift, moe_gain, moe_shift, router, up_weight, down_weight)))

    def forward_fn(*pieces):
        return forward(*pieces, expert_ids, priority)
    output, pullback, aux_values = jax.vjp(forward_fn, *floats, has_aux=True)
    gradients = pullback(cotangent.astype(jnp.float32))
    branch, middle, mixture = aux_values
    squares = jnp.stack([jnp.mean(value * value) for value in (floats[0], branch, middle, mixture, output)])
    return (output.astype(jnp.bfloat16), gradients[0].astype(jnp.bfloat16), gradients[1], gradients[2], gradients[3], gradients[4], gradients[5], gradients[6], gradients[7], gradients[8], gradients[9], jnp.sqrt(squares))
```

```python
import jax
import jax.numpy as jnp
from jax import lax
from jax.experimental import pallas as pl
from jax.experimental.pallas import tpu as pltpu
from jax.sharding import PartitionSpec as P


D = 512
HDIM = 64
SEQ = 197
E_DEV = 2
TOPK = 2
epsilon = 1e-06
BF = jnp.bfloat16
F32 = jnp.float32
PLANE = ("dp", "row")


def round_up(value, step):
    return -(-value // step) * step


def swap(value, axis, offset):
    size = lax.axis_size(axis)
    return lax.ppermute(value, axis, [(i, i ^ offset) for i in range(size)])


def exchange(pieces, axis):
    return [pieces[0]] + [swap(pieces[s], axis, s) for s in range(1, len(pieces))]


def share(value, axis):
    return exchange([value] * lax.axis_size(axis), axis)


def nn(a, b):
    return jnp.dot(a, b, preferred_element_type=F32)


def nt(a, b):
    return lax.dot_general(a, b, (((1,), (1,)), ((), ())), preferred_element_type=F32)


def tn(a, b):
    return lax.dot_general(a, b, (((0,), (0,)), ((), ())), preferred_element_type=F32)


def plane_size():
    return lax.axis_size("dp") * lax.axis_size("row")


def plane_gather(block):
    count = plane_size()
    if count > 8:
        return [lax.all_gather(block, PLANE, axis=0)]
    far = [block] + [swap(block, PLANE, s) for s in range(2, count, 2)]
    far = jnp.stack(far)
    near = swap(far, PLANE, 1)
    return [far, near]


def plane_reduce(parts, pack):
    if len(parts) == 1:
        total = jnp.sum(lax.all_to_all(parts[0], PLANE, 0, 0, tiled=True).astype(F32), axis=0)
        return total[0], [total[1]]
    got = swap(parts[1], PLANE, 1)
    pieces = []
    for k in (0, 1):
        near = parts[0][:, k] + got[:, k].astype(F32)
        packed = pack(near[1:]) if k == 0 else near[1:].astype(BF)
        pieces.append([near[0]] + [swap(packed[s - 1], PLANE, 2 * s) for s in range(1, near.shape[0])])
    return add_up(pieces[0]), pieces[1]


def add_up(pieces):
    total = pieces[0]
    for piece in pieces[1:]:
        total = total + piece.astype(F32)
    return total


PER_STEP = 2


def expert_kernel(*refs, n_groups, n_col, step_counts, tail):
    x_refs, go_refs = refs[:n_groups], refs[n_groups : 2 * n_groups]
    refs = refs[2 * n_groups :]
    w_refs, (sel_ref,) = refs[:n_col], refs[n_col : n_col + 1]
    refs = refs[n_col + 1 :]
    out_refs, own_ref = refs[:n_groups], refs[n_groups]
    send_refs = refs[n_groups + 1 : n_groups + n_col]
    w_all, grads = refs[n_groups + n_col :]
    step = pl.program_id(0)
    width = w_refs[0].shape[1]
    rows = x_refs[0].shape[1]
    lanes = min(round_up(rows, 128), x_refs[0].shape[2])

    @pl.when(step == 0)
    def _():
        for s in range(n_col):
            w_all[:, pl.ds(s * width, width), :] = w_refs[s][...]
        grads[...] = jnp.zeros_like(grads)

    if n_groups == 2:
        first = step < step_counts[0]
        x = jnp.where(first, x_refs[0][...], x_refs[1][...])
        go = jnp.where(first, go_refs[0][...], go_refs[1][...])
    else:
        x, go = x_refs[0][...], go_refs[0][...]
    start = rows - tail
    x_tail = x[:, start:, :lanes]
    gate = jnp.concatenate(
        [tn(x_tail[b], sel_ref[0] + sel_ref[1])[:rows] for b in range(PER_STEP)], axis=0)
    x = x.reshape(PER_STEP * rows, -1)
    go = go.reshape(PER_STEP * rows, -1)
    up, down = w_all[0], w_all[1]
    pre = nn(x, up)
    back = nn(go, down)
    cdf = 0.5 * (1.0 + lax.erf(pre * (0.5**0.5)))
    slope = cdf + pre * (jnp.exp(-0.5 * pre * pre) * ((2.0 * jnp.pi) ** -0.5))
    hidden = pre * cdf
    product = hidden.astype(BF).astype(F32) * back
    gated = (gate * hidden).astype(BF)
    grad_pre = (gate * back * slope).astype(BF)
    grads[0] += tn(x, grad_pre)
    grads[1] += tn(go, gated)
    mix = nt(gated, down).reshape(PER_STEP, rows, -1)
    grad_x = nt(grad_pre, up).reshape(PER_STEP, rows, -1)
    p_high = product.astype(BF)
    p_low = (product - p_high.astype(F32)).astype(BF)

    def gate_rows(which, b):
        part = pl.ds(b * rows, rows)
        high, low = p_high[b * rows : (b + 1) * rows], p_low[b * rows : (b + 1) * rows]
        return nt(sel_ref[which], high) + nt(sel_ref[which], low)

    def spread(value):
        missing = x_refs[0].shape[2] - rows
        return jnp.concatenate([value, jnp.zeros((tail, missing), F32)], axis=1)

    def store(k, packed):
        out_refs[k][:, 1] = mix.astype(out_refs[k].dtype)
        out_refs[k][:, 0, :start] = grad_x[:, :start].astype(out_refs[k].dtype)
        for b in range(PER_STEP):
            high = spread(gate_rows(0, b))
            if packed:
                low = spread(gate_rows(1, b))
                low = low - low.astype(BF).astype(F32)
                value = (grad_x[b, start:] + high).astype(BF) + low.astype(BF)
            else:
                value = grad_x[b, start:] + high
            out_refs[k][b, 0, start:] = value

    if n_groups == 2:
        pl.when(first)(lambda: store(0, False))
        pl.when(jnp.logical_not(first))(lambda: store(1, True))
    else:
        store(0, True)

    @pl.when(step == sum(step_counts) - 1)
    def _():
        own_ref[...] = grads[:, :width]
        for s in range(1, n_col):
            send_refs[s - 1][...] = grads[:, s * width : (s + 1) * width].astype(BF)


def run_experts(x_groups, go_groups, weights, select, interpret=False):
    n_groups, n_col = len(x_groups), len(weights)
    _, rows, model = x_groups[0].shape
    tail = select.shape[1]
    counts = [g.shape[0] // PER_STEP for g in x_groups]
    firsts = [sum(counts[:k]) for k in range(n_groups)]
    _, width, wide = weights[0].shape

    def blocks(k, *extra):
        low, high = firsts[k], counts[k] - 1
        rest = (0,) * (len(extra) + 2)
        return pl.BlockSpec((PER_STEP, *extra, rows, model), lambda i: (jnp.clip(i - low, 0, high), *rest))

    def fixed(shape):
        return pl.BlockSpec(shape, lambda i: (0,) * len(shape))

    def kind(k):
        return BF if k == n_groups - 1 else F32

    total = sum(g.shape[0] for g in x_groups)
    w_shape = (2, width, wide)
    out = pl.pallas_call(
        lambda *refs: expert_kernel(
            *refs, n_groups=n_groups, n_col=n_col, step_counts=counts, tail=tail),
        name="experts",
        grid=(sum(counts),),
        in_specs=[blocks(k) for k in range(n_groups)] * 2 + [fixed(w_shape)] * n_col + [fixed(select.shape)],
        out_specs=[blocks(k, 2) for k in range(n_groups)] + [fixed(w_shape)] * n_col,
        out_shape=[jax.ShapeDtypeStruct((g.shape[0], 2, rows, model), kind(k)) for k, g in enumerate(x_groups)]
        + [jax.ShapeDtypeStruct(w_shape, F32)] + [jax.ShapeDtypeStruct(w_shape, BF)] * (n_col - 1),
        scratch_shapes=[pltpu.VMEM((2, model, wide), BF), pltpu.VMEM((2, model, wide), F32)],
        cost_estimate=pl.CostEstimate(
            flops=12 * total * rows * model * wide, transcendentals=total * rows * wide,
            bytes_accessed=12 * total * rows * model),
        interpret=interpret,
    )(*x_groups, *go_groups, *weights, select)
    return out[:n_groups], out[n_groups], out[n_groups + 1 :]


def norm_stats(values):
    center = values - jnp.mean(values, axis=1, keepdims=True)
    inverse = lax.rsqrt(jnp.mean(center * center, axis=1, keepdims=True) + epsilon)
    return center * inverse, inverse


def norm_backward(grad_normed, normed, inverse, gain):
    scaled = grad_normed * gain
    grad_values = inverse * (
        scaled
        - jnp.mean(scaled, axis=1, keepdims=True)
        - normed * jnp.mean(scaled * normed, axis=1, keepdims=True)
    )
    return grad_values, jnp.sum(grad_normed * normed, axis=0), jnp.sum(grad_normed, axis=0)


def kept_pairs(choice_ids, order, own_first, own_count, experts, capacity):
    count = order.shape[0]
    numbers = jnp.arange(count, dtype=jnp.int32)
    lanes = jnp.arange(experts, dtype=jnp.int32)[None, :]
    hot_one = (choice_ids[:, 0:1] == lanes).astype(BF)
    hot_two = (choice_ids[:, 1:2] == lanes).astype(BF)
    pick = (order[:, None] == numbers[None, :]).astype(BF)
    ranked = nn(pick, jnp.concatenate([hot_one, hot_two], axis=1)).astype(BF)
    before = (numbers[:, None] > numbers[None, :]).astype(BF)
    earlier = nn(before, ranked)
    totals = jnp.sum(ranked[:, :experts].astype(F32), axis=0, keepdims=True)
    keep_one = ranked[:, :experts] * (earlier[:, :experts] < capacity).astype(BF)
    keep_two = ranked[:, experts:] * (earlier[:, experts:] + totals < capacity).astype(BF)
    own = own_first + jnp.arange(own_count, dtype=jnp.int32)
    pick_own = (own[:, None] == order[None, :]).astype(BF)
    return nn(pick_own, keep_one + keep_two)


def split_two(value):
    high = value.astype(BF)
    return high, (value - high.astype(F32)).astype(BF)


def body(
    tokens, cotangent, expert_ids, priority, qkv_weight, out_weight, attn_gain, attn_shift,
    moe_gain, moe_shift, router, up_weight, down_weight,
):
    rows_sh, width_c = tokens.shape
    n_dp = lax.axis_size("dp")
    n_col = lax.axis_size("col")
    n_row = lax.axis_size("row")
    c = lax.axis_index("col")
    experts = n_dp * E_DEV
    capacity = n_col * max(1, (5 * TOPK * rows_sh + 4 * experts * n_col - 1) // (4 * experts * n_col))
    own = rows_sh // n_col
    images = own // SEQ
    heads_r = qkv_weight.shape[2]
    heads = n_row * heads_r // HDIM
    ff = up_weight.shape[2]
    padded = round_up(own + 2 * experts, 16)
    gate_row = padded - 2 * experts
    score_scale = HDIM ** (-0.5)

    def to_rows(values):
        blocks = values.reshape(n_col, own, width_c)
        got = exchange([lax.dynamic_index_in_dim(blocks, c ^ s, 0, False) for s in range(n_col)], "col")
        return jnp.concatenate(got, axis=1)

    def to_slices(values):
        got = exchange([values[:, s * width_c : (s + 1) * width_c] for s in range(n_col)], "col")
        got = jnp.stack(got)
        return jnp.concatenate(
            [lax.dynamic_index_in_dim(got, c ^ s, 0, False) for s in range(n_col)], axis=0
        )

    stream = to_rows(tokens).astype(F32)

    small = jnp.concatenate(
        [jnp.stack([attn_gain, attn_shift, moe_gain, moe_shift]), router.T,
         jnp.zeros((round_up(4 + experts, 16) - 4 - experts, width_c), BF)], axis=0)
    block = jnp.concatenate(
        [qkv_weight[:, 0], qkv_weight[:, 1], qkv_weight[:, 2], out_weight, small], axis=0)
    by_col = jnp.stack(share(block, "col"))
    small_all = jnp.concatenate([by_col[s, 4 * width_c :] for s in range(n_col)], axis=1).astype(F32)
    g_one, b_one, g_two, b_two = (small_all[i : i + 1] for i in range(4))
    w_router = small_all[4 : 4 + experts].astype(BF)

    grad_out = to_rows(cotangent)
    grad_groups = plane_gather(jnp.pad(grad_out, ((0, padded - own), (0, 0))))
    grad_out = grad_out.astype(F32)

    mine = jnp.stack([up_weight.transpose(1, 0, 2).reshape(width_c, -1),
                      down_weight.transpose(2, 0, 1).reshape(width_c, -1)])
    mine, by_col = lax.optimization_barrier((mine, by_col))
    moe_weights = share(mine, "col")

    by_col = by_col[:, : 4 * width_c]
    by_row = [by_col] + [swap(by_col, "row", s) for s in range(2, n_row, 2)]
    by_row = jnp.stack(by_row)
    near_row = swap(by_row, "row", 1)
    by_row = jnp.stack([by_row, near_row], axis=1).reshape(n_row, n_col, 4, width_c, heads_r)
    w_qkv = by_row[:, :, :3].transpose(1, 3, 2, 0, 4).reshape(D, 3 * n_row * heads_r)
    w_out = by_row[:, :, 3].transpose(0, 2, 1, 3).reshape(n_row * heads_r, D)

    keep = kept_pairs(expert_ids, priority[0], c * own, own, experts, capacity)
    ids_own = lax.dynamic_slice_in_dim(expert_ids, c * own, own, 0)
    lanes = jnp.arange(experts, dtype=jnp.int32)[None, :]
    chosen = (ids_own[:, 0:1] == lanes) | (ids_own[:, 1:2] == lanes)

    normed_one, inverse_one = norm_stats(stream)
    first = (normed_one * g_one + b_one).astype(BF)
    qkv = nn(first, w_qkv).astype(BF).reshape(images, SEQ, 3, heads, HDIM)
    q, k, v = qkv[:, :, 0], qkv[:, :, 1], qkv[:, :, 2]
    scores = jnp.einsum("bqhd,bkhd->bhqk", q, k, preferred_element_type=F32) * score_scale
    raised = jnp.exp(scores - jnp.max(scores, axis=-1, keepdims=True))
    probs = raised / jnp.sum(raised, axis=-1, keepdims=True)
    probs_low = probs.astype(BF)
    attended = (
        jnp.einsum("bhqk,bkhd->bqhd", probs_low, v, preferred_element_type=F32).astype(BF).reshape(own, -1)
    )
    branch = nn(attended, w_out)
    middle = stream + branch
    normed_two, inverse_two = norm_stats(middle)
    second = (normed_two * g_two + b_two).astype(BF)
    logits = nt(second, w_router)
    top = jnp.max(jnp.where(chosen, logits, -jnp.inf), axis=1, keepdims=True)
    lifted = jnp.where(chosen, jnp.exp(jnp.where(chosen, logits - top, 0.0)), 0.0)
    gates = lifted / jnp.sum(lifted, axis=1, keepdims=True)
    gates_kept = gates * keep

    high, low = split_two(gates_kept.T)
    gate_block = jnp.pad(jnp.concatenate([high, low], axis=0), ((0, 0), (0, D - own)))
    block = jnp.concatenate(
        [second, jnp.zeros((gate_row - own, D), BF), gate_block], axis=0)
    x_groups = plane_gather(block)
    tail_start = gate_row // 16 * 16
    tail = padded - tail_start
    row_ids = jnp.arange(tail, dtype=jnp.int32)[:, None] - (gate_row - tail_start)
    expert_of = (
        lax.axis_index("dp") * E_DEV + jnp.arange(E_DEV * ff, dtype=jnp.int32)[None, :] // ff)
    select = jnp.stack([row_ids == expert_of, row_ids - experts == expert_of]).astype(BF)
    moe_sums, moe_own, moe_send = run_experts(x_groups, grad_groups, moe_weights, select)

    def pack_x(value):
        total = value[..., gate_row : gate_row + experts, :] + value[..., gate_row + experts :, :]
        high, low = split_two(total)
        return jnp.concatenate([value[..., :gate_row, :].astype(BF), high, low], axis=-2)

    got, mixture = plane_reduce(moe_sums, pack_x)
    gate_grad = (got[gate_row : gate_row + experts, :own] + got[gate_row + experts :, :own]).T * keep

    moe_got = [swap(moe_send[s - 1], "col", s) for s in range(1, n_col)]

    chosen_grad = gates * (gate_grad - jnp.sum(gates * gate_grad, axis=1, keepdims=True))
    logit_grad = chosen_grad.astype(BF)
    router_grad = tn(logit_grad, second)
    grad_second = got[:own] + nn(logit_grad, w_router)
    grad_norm, g_two_grad, b_two_grad = norm_backward(grad_second, normed_two, inverse_two, g_two)
    grad_middle = grad_out + grad_norm

    grad_branch = grad_middle.astype(BF)
    out_grad = tn(attended, grad_branch)
    grad_attended = nt(grad_branch, w_out).astype(BF).reshape(images, SEQ, heads, HDIM)
    grad_probs = jnp.einsum("bqhd,bkhd->bhqk", grad_attended, v, preferred_element_type=F32)
    grad_v = jnp.einsum("bhqk,bqhd->bkhd", probs_low, grad_attended, preferred_element_type=F32)
    grad_scores = (
        probs * (grad_probs - jnp.sum(probs * grad_probs, axis=-1, keepdims=True))
    ).astype(BF)
    grad_q = jnp.einsum("bhqk,bkhd->bqhd", grad_scores, k, preferred_element_type=F32) * score_scale
    grad_k = jnp.einsum("bhqk,bqhd->bkhd", grad_scores, q, preferred_element_type=F32) * score_scale
    grad_qkv = jnp.stack([grad_q, grad_k, grad_v], axis=2).astype(BF).reshape(own, -1)
    qkv_grad = tn(first, grad_qkv)
    grad_first = nt(grad_qkv, w_qkv)
    grad_norm, g_one_grad, b_one_grad = norm_backward(grad_first, normed_one, inverse_one, g_one)
    tokens_grad = to_slices((grad_middle + grad_norm).astype(BF))
    *mixture, _ = lax.optimization_barrier((*mixture, grad_first))
    mixture = add_up(mixture)[:own]
    output = middle + mixture
    block_out = to_slices(output.astype(BF))

    lane = jnp.arange(D, dtype=jnp.int32) % width_c
    squares = jnp.zeros((D,), F32)
    for i, value in enumerate((stream, branch, middle, mixture, output)):
        squares = squares + jnp.where(lane == i, jnp.sum(value * value), 0.0)
    n_small = round_up(5 + experts, 16)
    small = jnp.concatenate(
        [jnp.stack([g_one_grad, b_one_grad, g_two_grad, b_two_grad]), router_grad, squares[None],
         jnp.zeros((n_small - 5 - experts, D), F32)], axis=0)
    small = jnp.stack([small[:, t * width_c : (t + 1) * width_c] for t in range(n_col)])
    big = jnp.concatenate(
        [qkv_grad.reshape(n_col, width_c, 3, n_row, heads_r).transpose(3, 0, 2, 1, 4),
         out_grad.reshape(n_row, heads_r, n_col, width_c).transpose(0, 2, 1, 3)[:, :, None]], axis=2)
    big = big.reshape(n_row, n_col, 4 * width_c, heads_r)

    def send(big_part, small_part, axis, offset):
        high, low = split_two(small_part)
        message = jnp.concatenate(
            [big_part.astype(BF).reshape(-1, heads_r), high.reshape(-1, heads_r), low.reshape(-1, heads_r)],
            axis=0)
        got = swap(message, axis, offset).astype(F32)
        n_big = big_part.size // heads_r
        n_part = small_part.size // heads_r
        return (got[:n_big].reshape(big_part.shape),
                (got[n_big : n_big + n_part] + got[n_big + n_part :]).reshape(small_part.shape))

    bit = 1
    while bit < n_row:
        halves = big.reshape(big.shape[0] // 2, 2, *big.shape[1:])
        got_big, got_small = send(halves[:, 1], small, "row", bit)
        big, small = halves[:, 0] + got_big, small + got_small
        bit *= 2
    *moe_got, big = lax.optimization_barrier((*moe_got, big))
    moe_total = add_up([moe_own, *moe_got])
    up_grad = moe_total[0].reshape(width_c, E_DEV, ff).transpose(1, 0, 2)
    down_grad = moe_total[1].reshape(width_c, E_DEV, ff).transpose(1, 2, 0)
    big = big[0]
    total_big, total_small = big[0], small[0]
    for s in range(1, n_col):
        got_big, got_small = send(big[s], small[s], "col", s)
        total_big, total_small = total_big + got_big, total_small + got_small
    bit = 1
    while bit < n_dp:
        got_big, got_small = send(total_big, total_small, "dp", bit)
        total_big, total_small = total_big + got_big, total_small + got_small
        bit *= 2
    total_big = total_big.reshape(4, width_c, heads_r)
    qkv_grad = total_big[:3].transpose(1, 0, 2)
    out_grad = total_big[3]
    entries = own * D * n_dp * n_row * n_col
    stream_rms = jnp.sqrt(total_small[4 + experts, :5] / entries)
    return (
        block_out, tokens_grad, qkv_grad, out_grad, total_small[0], total_small[1], total_small[2],
        total_small[3], total_small[4 : 4 + experts].T, up_grad, down_grad, stream_rms,
    )


def solution(mesh):
    in_specs = (
        P(("dp", "row"), "col"), P(("dp", "row"), "col"), P(("dp", "row"), None), P(("dp", "row"), None),
        P("col", None, "row"), P("row", "col"), P("col"), P("col"), P("col"), P("col"), P("col", None),
        P("dp", "col", "row"), P("dp", "row", "col"),
    )
    out_specs = (
        P(("dp", "row"), "col"), P(("dp", "row"), "col"), P("col", None, "row"), P("row", "col"),
        P("col"), P("col"), P("col"), P("col"), P("col", None), P("dp", "col", "row"),
        P("dp", "row", "col"), P(),
    )

    return jax.shard_map(body, mesh=mesh, in_specs=in_specs, out_specs=out_specs, check_vma=False)
```
